32 devices in a mesh: dir: 2 (over x), sx: 4 (over y, core), sy: 4 (over z).
Axes of the slice: x: 2, y: 2, z: 4, core: 2. Of those that a mesh axis runs over, the one named last changes fastest.
Arguments:
- signs_x: int32 [2, 256], P('dir', 'sx'), may hold values from -2147483648 to 2147483647, as said below
- signs_y: int32 [2, 512], P('dir', 'sy'), may hold values from -2147483648 to 2147483647, as said below
- heights: int32 [256, 512], P('sx', 'sy'), may hold values from 0 to 63
- velocity: float32 [256, 512], P('sx', 'sy'), may hold values from 1 to 2
- background: float32 [2, 256, 512], P('dir', 'sx', 'sy'), may hold values from -4 to 4
Outputs:
- basis: float32 [64, 256, 512], P('dir', 'sx', 'sy')
- factor: float32 [64, 64], P('dir')
The draws below stay inside these ranges and needn't reach their ends.
Inputs may be any that keep to these rules, and one draw needn't show every extreme that they name: `signs_x`: packed sign words, every bit pattern possible. `signs_y`: packed sign words, every bit pattern possible.
All inputs are finite; a program needn't handle non-finite values.
Results may differ from the reference program's by a relative error of at most 0.00027.
Values sent between devices are 32-bit elements; how exact they have to be, the bound alone decides.
A program may use at most 64 MiB of HBM per device.

```python
import math
import jax
import jax.numpy as jnp
from jax import lax

PROBES = 32
LEVELS = 64
SHOTS = 2
DIRS = 64
NX = 256
NY = 512
N_DIR = 2


def packed_words(key, salt, length, flip_terms):
    base_words = jax.random.randint(jax.random.fold_in(key, salt), (1, length), -2147483648, 2147483647, dtype=jnp.int32)
    flips = jax.random.randint(jax.random.fold_in(key, salt + 1), (SHOTS, length), -2147483648, 2147483647, dtype=jnp.int32)
    for extra in range(flip_terms - 1):
        more = jax.random.randint(jax.random.fold_in(key, salt + 2 + extra), (SHOTS, length), -2147483648, 2147483647, dtype=jnp.int32)
        flips = flips & more
    return jnp.bitwise_xor(base_words, flips)


def draw_signs_x(key, part):
    return packed_words(key, 101, NX, 2)


def draw_signs_y(key, part):
    return packed_words(key, 211, NY, 3)


def draw_background(key, part):
    common_key = jax.random.fold_in(key, 307)
    own_key = jax.random.fold_in(key, 311)
    common = jax.random.normal(common_key, (1, NX, NY), jnp.float32)
    own = jax.random.normal(own_key, (SHOTS, NX, NY), jnp.float32)
    mixed = 0.8 * common + 0.6 * own
    return jnp.clip(mixed, -4.0, 4.0).astype(jnp.float32)


def place_ends(result, key, smallest, largest):
    longest = result.shape.index(max(result.shape))
    spots = []
    for shift in (0, 1):
        where = [jax.random.randint(jax.random.fold_in(key, axis), (), 0, length) for axis, length in enumerate(result.shape)]
        where[longest] = (where[longest] + shift) % result.shape[longest]
        spots.append(tuple(where))
    return result.at[spots[0]].set(smallest).at[spots[1]].set(largest)


def steps_of(key, dims, split, low, high):
    loudness = 1.0
    for axis_at, blocks in split:
        steps = jax.random.uniform(jax.random.fold_in(jax.random.fold_in(key, 6), axis_at), (blocks,), jnp.float32, low / len(split), high / len(split))
        loudness = loudness * jnp.repeat(jnp.exp(steps), dims[axis_at] // blocks).reshape((-1,) + (1,) * (len(dims) - 1 - axis_at))
    return loudness


def setup_inputs(seed: int = 0) -> dict:
    streams_of = jax.random.split(jax.random.key(seed), 6)
    return {
        "signs_x": draw_signs_x(jax.random.fold_in(streams_of[5], 71), 0),
        "signs_y": draw_signs_y(jax.random.fold_in(streams_of[5], 71), 0),
        "heights": place_ends(jax.random.randint(streams_of[2], (NX, NY), 0, LEVELS), jax.random.fold_in(streams_of[2], 1), 0, LEVELS - 1).astype(jnp.int32),
        "velocity": jnp.clip(jnp.exp(math.log(2.0) - 0.6931472 * jax.random.uniform(streams_of[3], (NX, NY), jnp.float32) ** steps_of(streams_of[3], (NX, NY), ((0, 4), (1, 4)), -0.2, 0.2)), 1.0, 2.0),
        "background": draw_background(jax.random.fold_in(streams_of[5], 71), 0),
    }


tau_step = 0.02

def unpack_signs(packed, per_group):
    bit_index = jnp.arange(per_group, dtype=jnp.int32)
    bit_values = jnp.right_shift(packed[:, None, :], bit_index[None, :, None]) & 1
    signed = (2 * bit_values - 1).astype(jnp.float32)
    return signed.reshape(packed.shape[0] * per_group, packed.shape[1])

def apply_step(wavefield, stiffness):
    weighted = stiffness * wavefield
    padded = jnp.pad(weighted, ((0, 0), (1, 1), (1, 1)))
    laplace = padded[:, 2:, 1:-1] + padded[:, :-2, 1:-1] + padded[:, 1:-1, 2:] + padded[:, 1:-1, :-2] - 4.0 * weighted
    return wavefield + tau_step * stiffness * laplace

def reference(signs_x, signs_y, heights, velocity, background):
    first_signs = unpack_signs(signs_x, PROBES)
    second = unpack_signs(signs_y, PROBES)
    kronecker = first_signs[:, :, None] * second[:, None, :]
    rolled = jnp.roll(kronecker.reshape(N_DIR, PROBES, NX, NY), -1, axis=1).reshape(DIRS, NX, NY)
    probe_dirs = kronecker + 0.5 * rolled
    stiffness = velocity * jnp.sqrt(1.0 + heights.astype(jnp.float32) / LEVELS)
    shot_fields = jnp.repeat(background, PROBES, axis=0)
    wavefield = shot_fields * probe_dirs
    for repeat in range(4):
        wavefield = apply_step(wavefield, stiffness[None])
    response = (shot_fields * wavefield).reshape(DIRS, NX * NY)
    gram_matrix = jnp.dot(response.astype(jnp.float32), response.T.astype(jnp.float32), precision=lax.Precision.HIGHEST, preferred_element_type=jnp.float32)
    factor_low = jnp.linalg.cholesky(gram_matrix)
    orthonormal = lax.linalg.triangular_solve(factor_low, response, left_side=True, lower=True)
    cell_count = math.sqrt(NX * NY)
    basis = (orthonormal * cell_count).reshape(DIRS, NX, NY)
    factor = factor_low.T / cell_count
    return (basis, factor)
```

```python
import functools
import math

import jax
import jax.numpy as jnp
from jax import lax
from jax.experimental import pallas as pl
from jax.experimental.pallas import tpu as pltpu
from jax.sharding import PartitionSpec as P

PROBES = 32
LEVELS = 64
TAU = 0.02
STEPS = 4
SUB = 8
GROUP = 16
UNROLL = 4
MESH = pl.DeviceIdType.MESH
OFFS = [(dx, dy) for dx in (-1, 0, 1) for dy in (-1, 0, 1)]
SLOT = {o: n for n, o in enumerate(OFFS)}
HIGH = lax.Precision.HIGHEST
F32 = jnp.float32
BF16 = jnp.bfloat16


def kernel(S, NX, NY, X, Y, sx_ref, sy_ref, h_ref, v_ref, b_ref, out_ref, fac_ref,
           pk, rc, aext, qext, pext, cc, sxw, fy, fyn, rbuf, xb, gx, gy, aug,
           send_sem, recv_sem, gxs, gxr, gys, gyr):
    D = S * PROBES
    E = X + 2 * SUB
    md = lax.axis_index("dir")
    mx = lax.axis_index("sx")
    my = lax.axis_index("sy")
    lane8 = lax.broadcasted_iota(jnp.int32, (SUB, Y), 1)

    def conds(dx, dy):
        out = []
        for c, o, n in ((mx, dx, NX), (my, dy, NY)):
            if o > 0:
                out.append(c < n - o)
            elif o < 0:
                out.append(c >= -o)
        return out

    def there(dx, dy):
        flags = conds(dx, dy)
        return flags[0] if len(flags) == 1 else jnp.logical_and(*flags)

    def when(flags, f):
        if not flags:
            f()
        elif len(flags) == 1:
            pl.when(flags[0])(f)
        else:
            pl.when(flags[0])(lambda: when(flags[1:], f))

    def device(d, dx, dy):
        return (d, lax.rem(mx + (dx + NX), NX), lax.rem(my + (dy + NY), NY))

    def of_message(d, dx, dy):
        return [md != d] if (dx, dy) == (0, 0) else conds(dx, dy)

    barrier = pltpu.get_barrier_semaphore()
    count = jnp.int32(0)

    def greet(flags, d, dx, dy):
        when(flags, lambda: pl.semaphore_signal(
            barrier, inc=1, device_id=device(d, dx, dy), device_id_type=MESH))
        one = jnp.int32(1)
        for flag in flags:
            one = one * jnp.where(flag, 1, 0)
        return one

    for d in range(S):
        for dx, dy in OFFS:
            count += greet(of_message(d, dx, dy), d, dx, dy)
    for k in range(2, NX):
        for dx in (k, -k):
            count += greet(conds(dx, 0), md, dx, 0)
    for k in range(2, NY):
        for dy in (k, -k):
            count += greet(conds(0, dy), md, 0, dy)

    stiff = v_ref[...] * jnp.sqrt(1.0 + h_ref[...].astype(F32) / LEVELS)
    sq = stiff * stiff
    a = stiff * b_ref[0]
    q = TAU * sq
    SG, EW, NT, SG2, NB = X, X + 8, X + 16, X + 32, X + 40
    pk[0:X, :] = a
    for base in (SG, SG2):
        syv = sy_ref[...]
        sxv = sx_ref[...]
        pk[base:base + 1, :] = (syv >> 16).astype(F32)
        pk[base + 1:base + 2, :] = (syv & 0xFFFF).astype(F32)
        pk[base + 2:base + 3, 0:X] = (sxv >> 16).astype(F32)
        pk[base + 3:base + 4, 0:X] = (sxv & 0xFFFF).astype(F32)
    edge = jnp.zeros((SUB, Y), F32)
    for r in range(X // SUB):
        ar = a[r * SUB:(r + 1) * SUB]
        qr = q[r * SUB:(r + 1) * SUB]
        t = jnp.where(jnp.logical_or(lane8 < 4, lane8 >= Y - 4), ar,
                      jnp.where(lane8 < 8, pltpu.roll(qr, 4, 1), pltpu.roll(qr, Y - 4, 1)))
        t = pltpu.roll(t, (16 * r + 8) % Y, 1)
        edge = jnp.where((lane8 >> 4) == r, t, edge)
    pk[EW:EW + 8, :] = edge
    pk[NT:NT + 8, :] = a[0:8]
    pk[NT + 8:NT + 16, :] = q[0:8]
    pk[NB:NB + 8, :] = a[X - 8:X]
    pk[NB + 8:NB + 16, :] = q[X - 8:X]

    def parts(dx, dy):
        if (dx, dy) == (0, 0):
            return 0, X + 8
        if dy == 0:
            return (NT, 24) if dx < 0 else (SG2, 24)
        return SG, 16

    pl.semaphore_wait(barrier, count)

    def copy_to(d, dx, dy):
        start, rows = parts(dx, dy)
        return pltpu.make_async_remote_copy(
            src_ref=pk.at[pl.ds(start, rows)],
            dst_ref=rc.at[md * 9 + SLOT[(-dx, -dy)], pl.ds(0, rows)],
            send_sem=send_sem.at[d * 9 + SLOT[(dx, dy)]],
            recv_sem=recv_sem.at[md * 9 + SLOT[(-dx, -dy)]],
            device_id=device(d, dx, dy), device_id_type=MESH)

    def each_message(f):
        for d in range(S):
            for dx, dy in OFFS:
                when(of_message(d, dx, dy), functools.partial(f, d, dx, dy))

    each_message(lambda d, dx, dy: copy_to(d, dx, dy).start())
    rc[md * 9 + SLOT[(0, 0)], 0:X + 8, :] = pk[0:X + 8, :]

    def wait_recv(s, dx, dy):
        start, rows = parts(-dx, -dy)
        pltpu.make_async_remote_copy(
            src_ref=pk.at[pl.ds(start, rows)],
            dst_ref=rc.at[s * 9 + SLOT[(dx, dy)], pl.ds(0, rows)],
            send_sem=send_sem.at[s * 9 + SLOT[(dx, dy)]],
            recv_sem=recv_sem.at[s * 9 + SLOT[(dx, dy)]],
            device_id=device(s, dx, dy), device_id_type=MESH).wait_recv()

    each_message(wait_recv)
    each_message(lambda d, dx, dy: copy_to(d, dx, dy).wait_send())

    lane1 = lax.broadcasted_iota(jnp.int32, (1, Y), 1)
    jv = lax.broadcasted_iota(jnp.int32, (PROBES, 2 * Y), 0)

    def masked(ok, val):
        return jnp.where(ok, val, jnp.zeros_like(val))

    def words(s, slot, base, row):
        hi = rc[s * 9 + slot, base + row:base + row + 1, :].astype(jnp.int32)
        lo = rc[s * 9 + slot, base + row + 1:base + row + 2, :].astype(jnp.int32)
        return (hi << 16) | lo

    def halo(s, dx, r):
        out = []
        for dy in (1, -1):
            pack = rc[s * 9 + SLOT[(dx, dy)], 8:16, :]
            out.append(masked(there(dx, dy), pltpu.roll(pack, (-(16 * r + 8)) % Y, 1)))
        e, w = out
        zero = jnp.zeros_like(e)
        ha = jnp.where(lane8 < 4, e, jnp.where(lane8 >= Y - 4, w, zero))
        hq = jnp.where(lane8 < 4, pltpu.roll(e, Y - 4, 1),
                       jnp.where(lane8 >= Y - 4, pltpu.roll(w, 4, 1), zero))
        return ha, hq

    def put_q(rows, cols, val):
        qext[cols, rows] = val
        pext[cols, rows] = 1.0 - 4.0 * val

    lo_c, hi_c = 0, 1
    put_q(slice(SUB, SUB + X), lo_c, q)
    for s in range(S):
        nslot, sslot = SLOT[(-1, 0)], SLOT[(1, 0)]
        aext[s, lo_c, SUB:SUB + X] = rc[s * 9 + SLOT[(0, 0)], 0:X, :]
        aext[s, lo_c, 0:SUB] = masked(there(-1, 0), rc[s * 9 + nslot, 8:16, :])
        aext[s, lo_c, SUB + X:E] = masked(there(1, 0), rc[s * 9 + sslot, 0:8, :])
        if s == 0:
            put_q(slice(0, SUB), lo_c, masked(there(-1, 0), rc[s * 9 + nslot, 16:24, :]))
            put_q(slice(SUB + X, E), lo_c, masked(there(1, 0), rc[s * 9 + sslot, 8:16, :]))
        groups = X // SUB
        for g in range(groups + 2):
            dx, r = (-1, groups - 1) if g == 0 else (1, 0) if g == groups + 1 else (0, g - 1)
            ha, hq = halo(s, dx, r)
            aext[s, hi_c, g * SUB:(g + 1) * SUB] = ha
            if s == 0:
                put_q(slice(g * SUB, (g + 1) * SUB), hi_c, hq)
        cc[s] = rc[s * 9 + SLOT[(0, 0)], 0:X, :] / sq
        wc = words(s, SLOT[(0, 0)], X, 0)
        we = words(s, SLOT[(0, 1)], 0, 0)
        ww = words(s, SLOT[(0, -1)], 0, 0)
        wide = jnp.concatenate([wc, jnp.where(lane1 < Y // 2, we, ww)], axis=1)
        wide = jnp.broadcast_to(wide, (PROBES, 2 * Y))
        fy[s * PROBES:(s + 1) * PROBES, :] = (2 * ((wide >> jv) & 1) - 1).astype(F32)
        fyn[s * PROBES:(s + 1) * PROBES, :] = 0.5 * (2 * ((wide >> ((jv + 1) & 31)) & 1) - 1).astype(F32)
        xc = words(s, SLOT[(0, 0)], X, 2)
        xn = words(s, nslot, 0, 2)
        xs = words(s, sslot, 16, 2)
        xw = jnp.where(lane1 < SUB, pltpu.roll(jnp.broadcast_to(xn, (SUB, Y)), (SUB - X) % Y, 1)[0:1],
                       jnp.where(lane1 < SUB + X, pltpu.roll(jnp.broadcast_to(xc, (SUB, Y)), SUB, 1)[0:1],
                                 pltpu.roll(jnp.broadcast_to(xs, (SUB, Y)), SUB + X, 1)[0:1]))
        sxw[s] = jnp.transpose(jnp.broadcast_to(xw, (Y, Y)))[0:E]

    j8 = lax.broadcasted_iota(jnp.int32, (GROUP, Y), 0)
    lane_g = lax.broadcasted_iota(jnp.int32, (GROUP, Y), 1)
    first_lane = lane_g == 0
    last_lane = lane_g == Y - 1

    def sides(m, h):
        ml, hl = pltpu.roll(m, 1, 1), pltpu.roll(h, 1, 1)
        mr, hr = pltpu.roll(m, Y - 1, 1), pltpu.roll(h, Y - 1, 1)
        return (jnp.where(first_lane, hl, ml) + jnp.where(last_lane, hr, mr),
                jnp.where(first_lane, ml, hl) + jnp.where(last_lane, mr, hr))

    def bc(ref, row, cols):
        return jnp.broadcast_to(ref[cols, pl.ds(row, 1), :], (GROUP, Y))

    def group(s, k):
        j0 = k * GROUP
        ja = j8 + j0
        jb = (ja + 1) & 31
        d0 = pl.multiple_of(s * PROBES + j0, GROUP)
        fyv = [fy[pl.ds(d0, GROUP), c * Y:(c + 1) * Y] for c in (lo_c, hi_c)]
        fynv = [fyn[pl.ds(d0, GROUP), c * Y:(c + 1) * Y] for c in (lo_c, hi_c)]

        def row(store, e, carry):
            wv = jnp.broadcast_to(sxw[s, pl.ds(e, 1), :], (GROUP, Y))
            fx = (2 * ((wv >> ja) & 1) - 1).astype(F32)
            fxn = (2 * ((wv >> jb) & 1) - 1).astype(F32)
            cur = tuple(
                jnp.broadcast_to(aext[s, c, pl.ds(e, 1), :], (GROUP, Y)) * (fx * fyv[n] + fxn * fynv[n])
                for n, c in enumerate((lo_c, hi_c)))
            new = []
            for t in range(STEPS):
                older, prev = carry[t]
                new.append((prev, cur))
                at = e - 1 - t
                sd = sides(*prev)
                cur = tuple(
                    bc(pext, at, c) * prev[n] + bc(qext, at, c) * (older[n] + cur[n] + sd[n])
                    for n, c in enumerate((lo_c, hi_c)))
            if store:
                i = e - STEPS - SUB
                rbuf[i, pl.ds(d0, GROUP), :] = cur[0] * jnp.broadcast_to(cc[s, pl.ds(i, 1), :], (GROUP, Y))
            return tuple(new)

        zero = fyv[0] * 0.0
        carry = tuple(((zero, zero), (zero, zero)) for _ in range(STEPS))
        begin = SUB - STEPS
        for e in range(begin, begin + 2 * STEPS):
            carry = row(False, e, carry)

        def rows(r, carry):
            for u in range(UNROLL):
                carry = row(True, r * UNROLL + (begin + 2 * STEPS + u), carry)
            return carry

        lax.fori_loop(0, X // UNROLL, rows, carry)

    for s in range(S):
        @pl.loop(0, PROBES // GROUP)
        def _(k):
            group(s, k)

    def inner(i, acc):
        x = jnp.concatenate([rbuf[2 * i], rbuf[2 * i + 1]], axis=1)
        hi = x.astype(BF16)
        lo = (x - hi.astype(F32)).astype(BF16)
        both = jnp.concatenate([hi, lo], axis=0)
        xb[i] = both
        new = lax.dot_general(both, both, (((1,), (1,)), ((), ())), preferred_element_type=F32)
        return new if acc is None else acc + new

    acc = lax.fori_loop(0, X // 2 - 1, lambda i, acc: inner(i + 1, acc), inner(0, None))
    acc = acc[0:D] + acc[D:2 * D]
    fold = 2 * D == Y
    if fold:
        acc = acc + pltpu.roll(acc, D, 1)
        lane_h = lax.broadcasted_iota(jnp.int32, (D // 2, Y), 1)
        gram = jnp.where(lane_h < D, acc[0:D // 2], acc[D // 2:D])
    else:
        gram = acc[:, 0:D] + acc[:, D:2 * D]

    def add_up(buf, mine, n, val, ssem, rsem, dest):
        buf[mine] = val

        def cp(to, slot):
            return pltpu.make_async_remote_copy(
                src_ref=buf.at[mine], dst_ref=buf.at[slot], send_sem=ssem.at[to],
                recv_sem=rsem.at[slot], device_id=dest(to), device_id_type=MESH)

        for to in range(n):
            pl.when(mine != to)(lambda: cp(to, mine).start())
        for frm in range(n):
            pl.when(mine != frm)(lambda: cp(frm, frm).wait_recv())
        for to in range(n):
            pl.when(mine != to)(lambda: cp(to, mine).wait_send())
        total = buf[0]
        for k in range(1, n):
            total = total + buf[k]
        return total

    gram = add_up(gx, mx, NX, gram, gxs, gxr, lambda k: (md, jnp.int32(k), my))
    gram = add_up(gy, my, NY, gram, gys, gyr, lambda k: (md, mx, jnp.int32(k)))

    wide_d = 2 * D
    la = lax.broadcasted_iota(jnp.int32, (D, wide_d), 1)
    ra = lax.broadcasted_iota(jnp.int32, (D, wide_d), 0)
    eye = (la == ra + D).astype(F32)
    if fold:
        full = jnp.concatenate([gram, pltpu.roll(gram, D, 1)], axis=0)
    else:
        full = jnp.concatenate([gram, gram], axis=1)
    mat = jnp.where(la < D, full, eye)
    sub8 = lax.broadcasted_iota(jnp.int32, (SUB, wide_d), 0)
    blocks = D // SUB
    for b in range(blocks):
        panel = mat[0:SUB]
        for t in range(SUB):
            prow = jnp.broadcast_to(panel[t:t + 1, :], (SUB, wide_d))
            col = b * SUB + t
            scale = lax.rsqrt(prow[:, col:col + 1])
            prow = prow * scale
            mult = panel[:, col:col + 1] * scale
            panel = jnp.where(sub8 == t, prow, jnp.where(sub8 > t, panel - mult * prow, panel))
        aug[b * SUB:(b + 1) * SUB, :] = panel
        if b + 1 < blocks:
            lhs = panel[:, 0:D]
            upd = lax.dot_general(lhs, panel, (((0,), (0,)), ((), ())), precision=HIGH,
                                  preferred_element_type=F32)
            mat = mat[SUB:] - upd[(b + 1) * SUB:]

    root = math.sqrt(X * Y * NX * NY)
    own = aug[pl.ds(pl.multiple_of(md * PROBES, PROBES), PROBES), :]
    lano = lax.broadcasted_iota(jnp.int32, own.shape, 1)
    orow = lax.broadcasted_iota(jnp.int32, own.shape, 0) + md * PROBES
    upper = jnp.where(lano >= orow, own, 0.0)
    fac_ref[...] = upper[:, 0:D] * (1.0 / root)
    linv = own[:, D:2 * D] * root
    l2 = jnp.concatenate([linv, linv], axis=1)
    l2h = l2.astype(BF16)
    l2l = (l2 - l2h.astype(F32)).astype(BF16)
    left = jnp.concatenate([l2h, l2l], axis=0)

    def final(i):
        y = lax.dot_general(left, xb[i], (((1,), (0,)), ((), ())), preferred_element_type=F32)
        y = y[0:PROBES] + y[PROBES:2 * PROBES]
        out_ref[:, 2 * i, :] = y[:, 0:Y]
        out_ref[:, 2 * i + 1, :] = y[:, Y:2 * Y]

    pl.loop(0, X // 2)(final)


def solution(mesh):
    S, NX, NY = (mesh.shape[k] for k in ("dir", "sx", "sy"))

    def shards(signs_x, signs_y, heights, velocity, background):
        X, Y = heights.shape
        D = S * PROBES
        E = X + 2 * SUB
        gshape = (D // 2, Y) if 2 * D == Y else (D, D)
        vm = pl.BlockSpec(memory_space=pltpu.VMEM)
        dma = pltpu.SemaphoreType.DMA
        return pl.pallas_call(
            functools.partial(kernel, S, NX, NY, X, Y),
            out_shape=(jax.ShapeDtypeStruct((PROBES, X, Y), F32), jax.ShapeDtypeStruct((PROBES, D), F32)),
            in_specs=[vm] * 5,
            out_specs=(vm, vm),
            scratch_shapes=[
                pltpu.VMEM((X + 56, Y), F32),
                pltpu.VMEM((S * 9, X + 8, Y), F32),
                pltpu.VMEM((S, 2, E, Y), F32),
                pltpu.VMEM((2, E, Y), F32),
                pltpu.VMEM((2, E, Y), F32),
                pltpu.VMEM((S, X, Y), F32),
                pltpu.VMEM((S, E, Y), jnp.int32),
                pltpu.VMEM((D, 2 * Y), F32),
                pltpu.VMEM((D, 2 * Y), F32),
                pltpu.VMEM((X, D, Y), F32),
                pltpu.VMEM((X // 2, 2 * D, 2 * Y), BF16),
                pltpu.VMEM((NX,) + gshape, F32),
                pltpu.VMEM((NY,) + gshape, F32),
                pltpu.VMEM((D, 2 * D), F32),
                dma((S * 9,)), dma((S * 9,)),
                dma((NX,)), dma((NX,)), dma((NY,)), dma((NY,)),
            ],
            compiler_params=pltpu.CompilerParams(
                collective_id=0, has_side_effects=True, vmem_limit_bytes=56 * 1024 * 1024),
        )(signs_x, signs_y, heights, velocity, background)

    in_specs = (P("dir", "sx"), P("dir", "sy"), P("sx", "sy"), P("sx", "sy"), P("dir", "sx", "sy"))
    out_specs = (P("dir", "sx", "sy"), P("dir", None))
    return jax.shard_map(shards, mesh=mesh, in_specs=in_specs, out_specs=out_specs, check_vma=False)
```

```python
import functools
import math

import jax
import jax.numpy as jnp
from jax import lax
from jax.experimental import pallas as pl
from jax.experimental.pallas import tpu as pltpu
from jax.sharding import PartitionSpec as P

PROBES = 32
LEVELS = 64
TAU = 0.02
STEPS = 4
SUB = 8
GROUP = 32
UNROLL = 8
MESH = pl.DeviceIdType.MESH
OFFS = [(dx, dy) for dx in (-1, 0, 1) for dy in (-1, 0, 1)]
SLOT = {o: n for n, o in enumerate(OFFS)}
HIGH = lax.Precision.HIGHEST
F32 = jnp.float32
BF16 = jnp.bfloat16


def kernel(S, NX, NY, X, Y, sx_ref, sy_ref, h_ref, v_ref, b_ref, out_ref, fac_ref,
           pk, rc, aext, qext, pext, cc, sxw, fy, fyn, rbuf, xb, gx, gy, aug,
           send_sem, recv_sem, gxs, gxr, gys, gyr):
    D = S * PROBES
    E = X + 2 * SUB
    md = lax.axis_index("dir")
    mx = lax.axis_index("sx")
    my = lax.axis_index("sy")
    lane8 = lax.broadcasted_iota(jnp.int32, (SUB, Y), 1)

    def conds(dx, dy):
        out = []
        for c, o, n in ((mx, dx, NX), (my, dy, NY)):
            if o > 0:
                out.append(c < n - o)
            elif o < 0:
                out.append(c >= -o)
        return out

    def there(dx, dy):
        flags = conds(dx, dy)
        return flags[0] if len(flags) == 1 else jnp.logical_and(*flags)

    def when(flags, f):
        if not flags:
            f()
        elif len(flags) == 1:
            pl.when(flags[0])(f)
        else:
            pl.when(flags[0])(lambda: when(flags[1:], f))

    def device(d, dx, dy):
        return (d, lax.rem(mx + (dx + NX), NX), lax.rem(my + (dy + NY), NY))

    def of_message(d, dx, dy):
        return [md != d] if (dx, dy) == (0, 0) else conds(dx, dy)

    barrier = pltpu.get_barrier_semaphore()
    count = jnp.int32(0)

    def greet(flags, d, dx, dy):
        when(flags, lambda: pl.semaphore_signal(
            barrier, inc=1, device_id=device(d, dx, dy), device_id_type=MESH))
        one = jnp.int32(1)
        for flag in flags:
            one = one * jnp.where(flag, 1, 0)
        return one

    for d in range(S):
        for dx, dy in OFFS:
            count += greet(of_message(d, dx, dy), d, dx, dy)
    for k in range(2, NX):
        for dx in (k, -k):
            count += greet(conds(dx, 0), md, dx, 0)
    for k in range(2, NY):
        for dy in (k, -k):
            count += greet(conds(0, dy), md, 0, dy)

    stiff = v_ref[...] * jnp.sqrt(1.0 + h_ref[...].astype(F32) / LEVELS)
    sq = stiff * stiff
    a = stiff * b_ref[0]
    q = TAU * sq
    SG, EW, NT, SG2, NB = X, X + 8, X + 16, X + 32, X + 40
    pk[0:X, :] = a
    for base in (SG, SG2):
        syv = sy_ref[...]
        sxv = sx_ref[...]
        pk[base:base + 1, :] = (syv >> 16).astype(F32)
        pk[base + 1:base + 2, :] = (syv & 0xFFFF).astype(F32)
        pk[base + 2:base + 3, 0:X] = (sxv >> 16).astype(F32)
        pk[base + 3:base + 4, 0:X] = (sxv & 0xFFFF).astype(F32)
    edge = jnp.zeros((SUB, Y), F32)
    for r in range(X // SUB):
        ar = a[r * SUB:(r + 1) * SUB]
        qr = q[r * SUB:(r + 1) * SUB]
        t = jnp.where(jnp.logical_or(lane8 < 4, lane8 >= Y - 4), ar,
                      jnp.where(lane8 < 8, pltpu.roll(qr, 4, 1), pltpu.roll(qr, Y - 4, 1)))
        t = pltpu.roll(t, (16 * r + 8) % Y, 1)
        edge = jnp.where((lane8 >> 4) == r, t, edge)
    pk[EW:EW + 8, :] = edge
    pk[NT:NT + 8, :] = a[0:8]
    pk[NT + 8:NT + 16, :] = q[0:8]
    pk[NB:NB + 8, :] = a[X - 8:X]
    pk[NB + 8:NB + 16, :] = q[X - 8:X]

    def parts(dx, dy):
        if (dx, dy) == (0, 0):
            return 0, X + 8
        if dy == 0:
            return (NT, 24) if dx < 0 else (SG2, 24)
        return SG, 16

    pl.semaphore_wait(barrier, count)

    def copy_to(d, dx, dy):
        start, rows = parts(dx, dy)
        return pltpu.make_async_remote_copy(
            src_ref=pk.at[pl.ds(start, rows)],
            dst_ref=rc.at[md * 9 + SLOT[(-dx, -dy)], pl.ds(0, rows)],
            send_sem=send_sem.at[d * 9 + SLOT[(dx, dy)]],
            recv_sem=recv_sem.at[md * 9 + SLOT[(-dx, -dy)]],
            device_id=device(d, dx, dy), device_id_type=MESH)

    def each_message(f):
        for d in range(S):
            for dx, dy in OFFS:
                when(of_message(d, dx, dy), functools.partial(f, d, dx, dy))

    each_message(lambda d, dx, dy: copy_to(d, dx, dy).start())
    rc[md * 9 + SLOT[(0, 0)], 0:X + 8, :] = pk[0:X + 8, :]

    def wait_recv(s, dx, dy):
        start, rows = parts(-dx, -dy)
        pltpu.make_async_remote_copy(
            src_ref=pk.at[pl.ds(start, rows)],
            dst_ref=rc.at[s * 9 + SLOT[(dx, dy)], pl.ds(0, rows)],
            send_sem=send_sem.at[s * 9 + SLOT[(dx, dy)]],
            recv_sem=recv_sem.at[s * 9 + SLOT[(dx, dy)]],
            device_id=device(s, dx, dy), device_id_type=MESH).wait_recv()

    each_message(wait_recv)
    each_message(lambda d, dx, dy: copy_to(d, dx, dy).wait_send())

    lane1 = lax.broadcasted_iota(jnp.int32, (1, Y), 1)
    jv = lax.broadcasted_iota(jnp.int32, (PROBES, 2 * Y), 0)

    def masked(ok, val):
        return jnp.where(ok, val, jnp.zeros_like(val))

    def words(s, slot, base, row):
        hi = rc[s * 9 + slot, base + row:base + row + 1, :].astype(jnp.int32)
        lo = rc[s * 9 + slot, base + row + 1:base + row + 2, :].astype(jnp.int32)
        return (hi << 16) | lo

    def halo(s, dx, r):
        out = []
        for dy in (1, -1):
            pack = rc[s * 9 + SLOT[(dx, dy)], 8:16, :]
            out.append(masked(there(dx, dy), pltpu.roll(pack, (-(16 * r + 8)) % Y, 1)))
        e, w = out
        zero = jnp.zeros_like(e)
        ha = jnp.where(lane8 < 4, e, jnp.where(lane8 >= Y - 4, w, zero))
        hq = jnp.where(lane8 < 4, pltpu.roll(e, Y - 4, 1),
                       jnp.where(lane8 >= Y - 4, pltpu.roll(w, 4, 1), zero))
        return ha, hq

    def put_q(rows, cols, val):
        qext[cols, rows] = val
        pext[cols, rows] = 1.0 - 4.0 * val

    lo_c, hi_c = 0, 1
    put_q(slice(SUB, SUB + X), lo_c, q)
    for s in range(S):
        nslot, sslot = SLOT[(-1, 0)], SLOT[(1, 0)]
        aext[s, lo_c, SUB:SUB + X] = rc[s * 9 + SLOT[(0, 0)], 0:X, :]
        aext[s, lo_c, 0:SUB] = masked(there(-1, 0), rc[s * 9 + nslot, 8:16, :])
        aext[s, lo_c, SUB + X:E] = masked(there(1, 0), rc[s * 9 + sslot, 0:8, :])
        if s == 0:
            put_q(slice(0, SUB), lo_c, masked(there(-1, 0), rc[s * 9 + nslot, 16:24, :]))
            put_q(slice(SUB + X, E), lo_c, masked(there(1, 0), rc[s * 9 + sslot, 8:16, :]))
        groups = X // SUB
        for g in range(groups + 2):
            dx, r = (-1, groups - 1) if g == 0 else (1, 0) if g == groups + 1 else (0, g - 1)
            ha, hq = halo(s, dx, r)
            aext[s, hi_c, g * SUB:(g + 1) * SUB] = ha
            if s == 0:
                put_q(slice(g * SUB, (g + 1) * SUB), hi_c, hq)
        cc[s] = rc[s * 9 + SLOT[(0, 0)], 0:X, :] / sq
        wc = words(s, SLOT[(0, 0)], X, 0)
        we = words(s, SLOT[(0, 1)], 0, 0)
        ww = words(s, SLOT[(0, -1)], 0, 0)
        wide = jnp.concatenate([wc, jnp.where(lane1 < Y // 2, we, ww)], axis=1)
        wide = jnp.broadcast_to(wide, (PROBES, 2 * Y))
        fy[s * PROBES:(s + 1) * PROBES, :] = (2 * ((wide >> jv) & 1) - 1).astype(F32)
        fyn[s * PROBES:(s + 1) * PROBES, :] = 0.5 * (2 * ((wide >> ((jv + 1) & 31)) & 1) - 1).astype(F32)
        xc = words(s, SLOT[(0, 0)], X, 2)
        xn = words(s, nslot, 0, 2)
        xs = words(s, sslot, 16, 2)
        xw = jnp.where(lane1 < SUB, pltpu.roll(jnp.broadcast_to(xn, (SUB, Y)), (SUB - X) % Y, 1)[0:1],
                       jnp.where(lane1 < SUB + X, pltpu.roll(jnp.broadcast_to(xc, (SUB, Y)), SUB, 1)[0:1],
                                 pltpu.roll(jnp.broadcast_to(xs, (SUB, Y)), SUB + X, 1)[0:1]))
        sxw[s] = jnp.transpose(jnp.broadcast_to(xw, (Y, Y)))[0:E]

    j8 = lax.broadcasted_iota(jnp.int32, (GROUP, Y), 0)
    lane_g = lax.broadcasted_iota(jnp.int32, (GROUP, Y), 1)
    first_lane = lane_g == 0
    last_lane = lane_g == Y - 1

    def sides(m, h):
        ml, hl = pltpu.roll(m, 1, 1), pltpu.roll(h, 1, 1)
        mr, hr = pltpu.roll(m, Y - 1, 1), pltpu.roll(h, Y - 1, 1)
        return (jnp.where(first_lane, hl, ml) + jnp.where(last_lane, hr, mr),
                jnp.where(first_lane, ml, hl) + jnp.where(last_lane, mr, hr))

    def bc(ref, row, cols):
        return jnp.broadcast_to(ref[cols, pl.ds(row, 1), :], (GROUP, Y))

    def group(s, k):
        j0 = k * GROUP
        ja = j8 + j0
        jb = (ja + 1) & 31
        d0 = pl.multiple_of(s * PROBES + j0, GROUP)
        fyv = [fy[pl.ds(d0, GROUP), c * Y:(c + 1) * Y] for c in (lo_c, hi_c)]
        fynv = [fyn[pl.ds(d0, GROUP), c * Y:(c + 1) * Y] for c in (lo_c, hi_c)]

        def row(store, e, carry):
            wv = jnp.broadcast_to(sxw[s, pl.ds(e, 1), :], (GROUP, Y))
            fx = (2 * ((wv >> ja) & 1) - 1).astype(F32)
            fxn = (2 * ((wv >> jb) & 1) - 1).astype(F32)
            cur = tuple(
                jnp.broadcast_to(aext[s, c, pl.ds(e, 1), :], (GROUP, Y)) * (fx * fyv[n] + fxn * fynv[n])
                for n, c in enumerate((lo_c, hi_c)))
            new = []
            for t in range(STEPS):
                older, prev = carry[t]
                new.append((prev, cur))
                at = e - 1 - t
                sd = sides(*prev)
                cur = tuple(
                    bc(pext, at, c) * prev[n] + bc(qext, at, c) * (older[n] + cur[n] + sd[n])
                    for n, c in enumerate((lo_c, hi_c)))
            if store:
                i = e - STEPS - SUB
                rbuf[i, pl.ds(d0, GROUP), :] = cur[0] * jnp.broadcast_to(cc[s, pl.ds(i, 1), :], (GROUP, Y))
            return tuple(new)

        zero = fyv[0] * 0.0
        carry = tuple(((zero, zero), (zero, zero)) for _ in range(STEPS))
        begin = SUB - STEPS
        for e in range(begin, begin + 2 * STEPS):
            carry = row(False, e, carry)

        def rows(r, carry):
            for u in range(UNROLL):
                carry = row(True, r * UNROLL + (begin + 2 * STEPS + u), carry)
            return carry

        lax.fori_loop(0, X // UNROLL, rows, carry)

    for s in range(S):
        @pl.loop(0, PROBES // GROUP)
        def _(k):
            group(s, k)

    def inner(i, acc):
        x = jnp.concatenate([rbuf[2 * i], rbuf[2 * i + 1]], axis=1)
        hi = x.astype(BF16)
        lo = (x - hi.astype(F32)).astype(BF16)
        both = jnp.concatenate([hi, lo], axis=0)
        xb[i] = both
        new = lax.dot_general(both, both, (((1,), (1,)), ((), ())), preferred_element_type=F32)
        return new if acc is None else acc + new

    per = 4

    def several(i, acc):
        for u in range(per):
            acc = inner(i * per + u, acc)
        return acc

    acc = lax.fori_loop(0, X // 2 // per - 1, lambda i, acc: several(i + 1, acc), several(0, None))
    acc = acc[0:D] + acc[D:2 * D]
    fold = 2 * D == Y
    if fold:
        acc = acc + pltpu.roll(acc, D, 1)
        lane_h = lax.broadcasted_iota(jnp.int32, (D // 2, Y), 1)
        gram = jnp.where(lane_h < D, acc[0:D // 2], acc[D // 2:D])
    else:
        gram = acc[:, 0:D] + acc[:, D:2 * D]

    def add_up(buf, mine, n, val, ssem, rsem, dest):
        buf[mine] = val

        def cp(to, slot):
            return pltpu.make_async_remote_copy(
                src_ref=buf.at[mine], dst_ref=buf.at[slot], send_sem=ssem.at[to],
                recv_sem=rsem.at[slot], device_id=dest(to), device_id_type=MESH)

        for to in range(n):
            pl.when(mine != to)(lambda: cp(to, mine).start())
        for frm in range(n):
            pl.when(mine != frm)(lambda: cp(frm, frm).wait_recv())
        for to in range(n):
            pl.when(mine != to)(lambda: cp(to, mine).wait_send())
        total = buf[0]
        for k in range(1, n):
            total = total + buf[k]
        return total

    gram = add_up(gx, mx, NX, gram, gxs, gxr, lambda k: (md, jnp.int32(k), my))
    gram = add_up(gy, my, NY, gram, gys, gyr, lambda k: (md, mx, jnp.int32(k)))

    wide_d = 2 * D
    la = lax.broadcasted_iota(jnp.int32, (D, wide_d), 1)
    ra = lax.broadcasted_iota(jnp.int32, (D, wide_d), 0)
    eye = (la == ra + D).astype(F32)
    if fold:
        full = jnp.concatenate([gram, pltpu.roll(gram, D, 1)], axis=0)
    else:
        full = jnp.concatenate([gram, gram], axis=1)
    mat = jnp.where(la < D, full, eye)
    sub8 = lax.broadcasted_iota(jnp.int32, (SUB, wide_d), 0)
    blocks = D // SUB
    for b in range(blocks):
        panel = mat[0:SUB]
        for t in range(SUB):
            prow = jnp.broadcast_to(panel[t:t + 1, :], (SUB, wide_d))
            col = b * SUB + t
            scale = lax.rsqrt(prow[:, col:col + 1])
            prow = prow * scale
            mult = panel[:, col:col + 1] * scale
            panel = jnp.where(sub8 == t, prow, jnp.where(sub8 > t, panel - mult * prow, panel))
        aug[b * SUB:(b + 1) * SUB, :] = panel
        if b + 1 < blocks:
            lhs = panel[:, 0:D]
            upd = lax.dot_general(lhs, panel, (((0,), (0,)), ((), ())), precision=HIGH,
                                  preferred_element_type=F32)
            mat = mat[SUB:] - upd[(b + 1) * SUB:]

    root = math.sqrt(X * Y * NX * NY)
    own = aug[pl.ds(pl.multiple_of(md * PROBES, PROBES), PROBES), :]
    lano = lax.broadcasted_iota(jnp.int32, own.shape, 1)
    orow = lax.broadcasted_iota(jnp.int32, own.shape, 0) + md * PROBES
    upper = jnp.where(lano >= orow, own, 0.0)
    fac_ref[...] = upper[:, 0:D] * (1.0 / root)
    linv = own[:, D:2 * D] * root
    l2 = jnp.concatenate([linv, linv], axis=1)
    l2h = l2.astype(BF16)
    l2l = (l2 - l2h.astype(F32)).astype(BF16)
    left = jnp.concatenate([l2h, l2l], axis=0)

    def final(i):
        y = lax.dot_general(left, xb[i], (((1,), (0,)), ((), ())), preferred_element_type=F32)
        y = y[0:PROBES] + y[PROBES:2 * PROBES]
        out_ref[:, 2 * i, :] = y[:, 0:Y]
        out_ref[:, 2 * i + 1, :] = y[:, Y:2 * Y]

    pl.loop(0, X // 2, unroll=8)(final)


def solution(mesh):
    S, NX, NY = (mesh.shape[k] for k in ("dir", "sx", "sy"))

    def shards(signs_x, signs_y, heights, velocity, background):
        X, Y = heights.shape
        D = S * PROBES
        E = X + 2 * SUB
        gshape = (D // 2, Y) if 2 * D == Y else (D, D)
        vm = pl.BlockSpec(memory_space=pltpu.VMEM)
        dma = pltpu.SemaphoreType.DMA
        return pl.pallas_call(
            functools.partial(kernel, S, NX, NY, X, Y),
            out_shape=(jax.ShapeDtypeStruct((PROBES, X, Y), F32), jax.ShapeDtypeStruct((PROBES, D), F32)),
            in_specs=[vm] * 5,
            out_specs=(vm, vm),
            scratch_shapes=[
                pltpu.VMEM((X + 56, Y), F32),
                pltpu.VMEM((S * 9, X + 8, Y), F32),
                pltpu.VMEM((S, 2, E, Y), F32),
                pltpu.VMEM((2, E, Y), F32),
                pltpu.VMEM((2, E, Y), F32),
                pltpu.VMEM((S, X, Y), F32),
                pltpu.VMEM((S, E, Y), jnp.int32),
                pltpu.VMEM((D, 2 * Y), F32),
                pltpu.VMEM((D, 2 * Y), F32),
                pltpu.VMEM((X, D, Y), F32),
                pltpu.VMEM((X // 2, 2 * D, 2 * Y), BF16),
                pltpu.VMEM((NX,) + gshape, F32),
                pltpu.VMEM((NY,) + gshape, F32),
                pltpu.VMEM((D, 2 * D), F32),
                dma((S * 9,)), dma((S * 9,)),
                dma((NX,)), dma((NX,)), dma((NY,)), dma((NY,)),
            ],
            compiler_params=pltpu.CompilerParams(
                collective_id=0, has_side_effects=True, vmem_limit_bytes=56 * 1024 * 1024),
        )(signs_x, signs_y, heights, velocity, background)

    in_specs = (P("dir", "sx"), P("dir", "sy"), P("sx", "sy"), P("sx", "sy"), P("dir", "sx", "sy"))
    out_specs = (P("dir", "sx", "sy"), P("dir", None))
    return jax.shard_map(shards, mesh=mesh, in_specs=in_specs, out_specs=out_specs, check_vma=False)
```
